32 devices in a mesh: group: 8 (over y, x, core), inst: 4 (over z).
Axes of the slice: x: 2, y: 2, z: 4, core: 2. Of those that a mesh axis runs over, the one named last changes fastest.
Arguments:
- old_cache: bfloat16 [4, 512, 16, 2048], P('inst', 'group'), may hold values from -64 to 64, as said below
- block_table: int32 [16, 128], replicated, may hold values from 0 to 511, as said below
- place_after: int32 [16], replicated, may hold values from 0 to 15, as said below
- context_len: int32 [16], replicated, may hold values from 256 to 2048
- queries: bfloat16 [4096, 4096], P(('group', 'inst')), may hold values from -64 to 64
- new_kv: bfloat16 [4096, 2048], P(('group', 'inst')), may hold values from -6 to 6
Outputs:
- attended: bfloat16 [4096, 4096], P(('group', 'inst'))
The draws below stay inside these ranges and needn't reach their ends.
Inputs may be any that keep to these rules, and one draw needn't show every extreme that they name: Each of old_cache and queries lies within the printed range. A permutation: request r moves to group index place_after[r] // 2, as that group's request number place_after[r] % 2. block_table[r, k] lies on the devices of inst index k // 32: on group index block_table[r, k] // 64, slot block_table[r, k] % 64. Every slot of every device holds exactly one block, and each device holds exactly 8 blocks of the requests of each new group.
All inputs are finite; a program needn't handle non-finite values.
Results may differ from the reference program's by a relative error of at most 0.0075.
Values may be sent and summed in bfloat16 or wider, within the bound.
No kernel may reach another device: no remote copies, remote signals or barrier semaphores. Data moves between devices by JAX's collectives and lax.ppermute only.
A program may use at most 128 MiB of HBM per device.

```python
import jax
import jax.numpy as jnp
from jax import lax

HQ = 32
KVH = 8
HD = 128
BLK = 16
CTX = 2048
PRE = 256
REQS = 16
NBLK = 128
NBI = 32
N_GROUP = 8
N_INST = 4


def layout_plan(key):
    rgroup = N_INST // 2
    reqs = rgroup * N_GROUP
    nblk = CTX // BLK
    per_inst = nblk // N_INST
    slots = rgroup * per_inst
    per_pair = slots // N_GROUP
    base = jax.random.fold_in(key, 101)
    after = jax.random.permutation(jax.random.fold_in(base, 1), reqs).astype(jnp.int32)
    request_of = jnp.argsort(after).astype(jnp.int32)
    item_keys = jax.random.split(jax.random.fold_in(base, 2), N_INST * N_GROUP)
    items = jax.vmap(lambda k: jax.random.permutation(k, slots))(item_keys).reshape(N_INST, N_GROUP, slots).astype(jnp.int32)
    slot_keys = jax.random.split(jax.random.fold_in(base, 3), N_INST * N_GROUP)
    sigma = jax.vmap(lambda k: jax.random.permutation(k, slots))(slot_keys).reshape(N_INST, N_GROUP, slots).astype(jnp.int32)
    position = jnp.arange(slots, dtype=jnp.int32)
    source = position // per_pair
    target = jnp.arange(N_GROUP, dtype=jnp.int32)
    local_pos = target[:, None] * per_pair + position[None, :] % per_pair
    inst_ids = jnp.arange(N_INST, dtype=jnp.int32)
    chosen = sigma[inst_ids[:, None, None], source[None, None, :], local_pos[None, :, :]]
    physical = source[None, None, :] * slots + chosen
    owner_req = request_of[target[None, :, None] * rgroup + items // per_inst]
    block_ids = inst_ids[:, None, None] * per_inst + items % per_inst
    table = jnp.zeros((reqs, nblk), jnp.int32).at[owner_req.ravel(), block_ids.ravel()].set(physical.ravel())
    return (after, table)


def draw_place_after(key, part):
    return layout_plan(key)[0]


def draw_block_table(key, part):
    return layout_plan(key)[1]


def draw_queries(key, part):
    rows = N_INST // 2 * N_GROUP * PRE
    values = jax.random.normal(jax.random.fold_in(key, 21), (rows, HQ * HD), jnp.float32)
    return jnp.clip(values, -64.0, 64.0).astype(jnp.bfloat16)


def draw_old_cache(key, part):
    shape = (N_INST, N_GROUP * (N_INST // 2) * (CTX // BLK // N_INST), BLK, 2 * KVH * HD)
    values = jax.random.normal(jax.random.fold_in(key, 31), shape, jnp.float32)
    return jnp.clip(values, -64.0, 64.0).astype(jnp.bfloat16)


def set_ends(array, rng, smallest, high):
    spot = [jax.random.randint(jax.random.fold_in(rng, axis), (), 0, length) for axis, length in enumerate(array.shape)]
    widest = array.shape.index(max(array.shape))
    neighbour = spot[:widest] + [(spot[widest] + 1) % array.shape[widest]] + spot[widest + 1:]
    return array.at[tuple(spot)].set(smallest).at[tuple(neighbour)].set(high)


def block_scale(own_key, shape, shards, low, high):
    loudness = 1.0
    for axis_at, parts in shards:
        steps = jax.random.uniform(jax.random.fold_in(jax.random.fold_in(own_key, 6), axis_at), (parts,), jnp.float32, low / len(shards), high / len(shards))
        loudness = loudness * jnp.repeat(jnp.exp(steps), shape[axis_at] // parts).reshape((-1,) + (1,) * (len(shape) - 1 - axis_at))
    return loudness


def noise(stream_key, dims, spread, bound, cuts=(), kind=jnp.bfloat16):
    values = spread * jax.random.normal(stream_key, dims, jnp.float32)
    if cuts:
        values = values * block_scale(stream_key, dims, cuts, -0.22, 0.18)
    return jnp.clip(values, -bound, bound).astype(kind)


def setup_inputs(seed: int = 0) -> dict:
    seeds = jax.random.split(jax.random.key(seed), 7)
    old_cache = draw_old_cache(jax.random.fold_in(seeds[6], 71), 0)
    block_table = draw_block_table(jax.random.fold_in(seeds[6], 71), 0)
    place_after = draw_place_after(jax.random.fold_in(seeds[6], 71), 0)
    context_len = set_ends(jax.random.randint(seeds[3], (REQS,), CTX // 8, CTX + 1), jax.random.fold_in(seeds[3], 1), CTX // 8, CTX).astype(jnp.int32)
    queries = draw_queries(jax.random.fold_in(seeds[6], 71), 0)
    new_kv = noise(seeds[5], (REQS * PRE, 2 * KVH * HD), 1.0, 6.0, ((0, 32),))
    return {"old_cache": old_cache, "block_table": block_table, "place_after": place_after, "context_len": context_len, "queries": queries, "new_kv": new_kv}


def reference(old_cache, block_table, place_after, context_len, queries, new_kv):
    request_of = jnp.argsort(place_after).astype(jnp.int32)
    groups = HQ // KVH
    inst_of = (jnp.arange(NBLK, dtype=jnp.int32) // NBI).astype(jnp.int32)

    def one_slot(slot):
        request = request_of[slot]
        length = context_len[request]
        blocks = old_cache[inst_of, block_table[request]]
        cache = blocks.reshape(CTX, 2 * KVH * HD)
        fresh = lax.dynamic_slice_in_dim(new_kv, (slot * PRE).astype(jnp.int32), PRE, 0)
        asked = lax.dynamic_slice_in_dim(queries, (slot * PRE).astype(jnp.int32), PRE, 0)
        keyvals = jnp.concatenate([cache, fresh], axis=0).astype(jnp.float32)
        keys = keyvals[:, :KVH * HD].reshape(CTX + PRE, KVH, HD)
        values = keyvals[:, KVH * HD:].reshape(CTX + PRE, KVH, HD)
        heads = asked.astype(jnp.float32).reshape(PRE, KVH, groups, HD)
        scores = jnp.einsum("qhgd,khd->hgqk", heads, keys) * (HD ** -0.5)
        key_index = jnp.arange(CTX + PRE, dtype=jnp.int32)
        query_index = jnp.arange(PRE, dtype=jnp.int32)
        allowed = jnp.where(key_index[None, :] < CTX, key_index[None, :] < length,
                            key_index[None, :] - CTX <= query_index[:, None])
        scores = jnp.where(allowed[None, None], scores, -jnp.inf)
        largest = jnp.max(scores, axis=-1, keepdims=True)
        weights = jnp.exp(scores - largest).astype(jnp.bfloat16).astype(jnp.float32)
        total = jnp.sum(weights, axis=-1)
        summed = jnp.einsum("hgqk,khd->hgqd", weights, values)
        result = summed / total[..., None]
        return jnp.transpose(result, (2, 0, 1, 3)).reshape(PRE, HQ * HD).astype(jnp.bfloat16)

    outputs = lax.map(one_slot, jnp.arange(REQS, dtype=jnp.int32))
    return outputs.reshape(REQS * PRE, HQ * HD)
```

```python
import functools
import math

import jax
import jax.numpy as jnp
from jax import lax
from jax.experimental import pallas as pl
from jax.experimental.pallas import tpu as pltpu
from jax.sharding import PartitionSpec as P

KVH = 8
HD = 128
NEG_FILL = -1e30
HEADS_PER_CHUNK = 2


SMEM = pl.BlockSpec(memory_space=pltpu.SMEM)
VMEM = pl.BlockSpec(memory_space=pltpu.VMEM)
ANY = pl.BlockSpec(memory_space=pl.ANY)


def pack_kernel(chunk, slots_ref, me_ref, cache_ref, *rest):
    outs, sems = rest[:-1], rest[-1]
    steps = len(outs)
    blk = cache_ref.shape[1]
    per_pair = outs[0].shape[0] // blk
    width = outs[0].shape[1] // 2
    me = me_ref[0]
    for step in range(steps):
        for item in range(per_pair):
            slot = slots_ref[(me ^ step) * per_pair + item]
            for part in range(2):
                pltpu.make_async_copy(
                    cache_ref.at[slot, :, pl.ds(part * KVH * HD + chunk * width, width)],
                    outs[step].at[pl.ds(item * blk, blk), pl.ds(part * width, width)],
                    sems.at[step],
                ).start()
    for step in range(steps):
        pltpu.make_async_copy(outs[step], outs[step], sems.at[step]).wait()


def pack(chunk, slots_table, me, cache, steps, gate):
    blk = cache.shape[1]
    per_pair = cache.shape[0] // steps
    width = 2 * HEADS_PER_CHUNK * HD
    piece = jax.ShapeDtypeStruct((per_pair * blk, width), cache.dtype)
    extra = [] if gate is None else [gate]

    def body(slots_ref, me_ref, cache_ref, *rest):
        pack_kernel(chunk, slots_ref, me_ref, cache_ref, *rest[len(extra) :])

    return pl.pallas_call(
        body,
        out_shape=[piece] * steps,
        in_specs=[SMEM, SMEM, ANY] + [ANY] * len(extra),
        out_specs=[VMEM] * steps,
        scratch_shapes=[pltpu.SemaphoreType.DMA((steps,))],
        cost_estimate=pl.CostEstimate(
            flops=0, bytes_accessed=2 * steps * piece.size * 2, transcendentals=0
        ),
        name="pack",
    )(slots_table, me, cache, *extra)


def unpack_kernel(steps, order_ref, which_ref, *rest):
    arrived = rest[:steps]
    outs = rest[steps:-2]
    held, sems = rest[-2:]
    blk = held.shape[1]
    per_pair = held.shape[0] // steps
    per_inst = outs[0].shape[0] // blk
    for step in range(steps):
        for item in range(per_pair):
            pltpu.make_async_copy(
                arrived[step].at[pl.ds(item * blk, blk)],
                held.at[step * per_pair + item],
                sems.at[step],
            ).start()
    for step in range(steps):
        span = held.at[pl.ds(step * per_pair, per_pair)]
        pltpu.make_async_copy(span, span, sems.at[step]).wait()
    for number, out in enumerate(outs):
        first = which_ref[number] * per_inst
        for item in range(per_inst):
            out[item * blk : (item + 1) * blk, :] = held[order_ref[first + item]]


def unpack(order, which, arrived, blk, pieces):
    steps = len(arrived)
    rows, width = arrived[0].shape
    slots = steps * rows // blk
    out = jax.ShapeDtypeStruct((order.shape[1] * blk, width), arrived[0].dtype)
    return pl.pallas_call(
        functools.partial(unpack_kernel, steps),
        out_shape=[out] * pieces,
        in_specs=[SMEM, SMEM] + [ANY] * steps,
        out_specs=[VMEM] * pieces,
        scratch_shapes=[
            pltpu.VMEM((slots, blk, width), arrived[0].dtype),
            pltpu.SemaphoreType.DMA((steps,)),
        ],
        cost_estimate=pl.CostEstimate(
            flops=0, bytes_accessed=2 * steps * rows * width * 2, transcendentals=0
        ),
        name="unpack",
    )(order.reshape(-1), which, *arrived)


def attend_kernel(groups, live_ref, own_q, other_q, new_k, new_v, *rest):
    pieces = rest[:-4]
    own_sum, own_stat, send_sum, send_stat = rest[-4:]
    tokens = own_q.shape[0]
    heads = new_k.shape[1] // HD
    factor = HD ** (-0.5) * math.log2(math.e)
    parity = live_ref[len(pieces)]
    rows = pieces[0].shape[0]
    spots = lax.broadcasted_iota(jnp.int32, (1, rows), 1)
    fills = [
        jnp.where(spots < live_ref[n], 0.0, NEG_FILL).astype(jnp.float32)
        for n in range(len(pieces))
    ]
    at_query = lax.broadcasted_iota(jnp.int32, (2 * tokens, tokens), 0)
    at_key = lax.broadcasted_iota(jnp.int32, (2 * tokens, tokens), 1)
    shift = jnp.where(parity == 0, 2 * tokens, -2 * tokens)
    reach = jnp.where(at_query < tokens, at_query, at_query + shift)
    fresh_fill = jnp.where(reach >= at_key, 0.0, NEG_FILL).astype(jnp.float32)
    lanes = lax.broadcasted_iota(jnp.int32, (2 * tokens, HD), 1)
    ones = jnp.ones((rows, HD), jnp.bfloat16)

    def one(number, stat):
        head = number // groups
        qcol = pl.ds(pl.multiple_of(number * HD, HD), HD)
        kcol = pl.ds(pl.multiple_of(head * HD, HD), HD)
        vcol = pl.ds(pl.multiple_of((heads + head) * HD, HD), HD)
        query = jnp.concatenate([own_q[:, qcol], other_q[:, qcol]], axis=0)
        contract = (((1,), (1,)), ((), ()))
        scores = [
            lax.dot_general(query, p[:, kcol], contract, preferred_element_type=jnp.float32) + f
            for p, f in zip(pieces, fills)
        ]
        scores.append(
            lax.dot_general(query, new_k[:, kcol], contract, preferred_element_type=jnp.float32)
            + fresh_fill
        )
        largest = functools.reduce(
            jnp.maximum, [jnp.max(s, axis=1, keepdims=True) for s in scores]
        )
        total = jnp.zeros((2 * tokens, 2 * HD), jnp.float32)
        values = [p[:, vcol] for p in pieces] + [new_v[:, kcol]]
        for s, v in zip(scores, values):
            weight = jnp.exp2((s - largest) * factor).astype(jnp.bfloat16)
            wide = jnp.concatenate([v, ones[: v.shape[0]]], axis=1)
            total += jnp.dot(weight, wide, preferred_element_type=jnp.float32)
        own_sum[:, qcol] = total[:tokens, :HD]
        send_sum[:, qcol] = total[tokens:, :HD].astype(jnp.bfloat16)
        stat = jnp.where(lanes == number, largest, stat)
        return jnp.where(lanes == HD // 2 + number, total[:, HD:], stat)

    stat = lax.fori_loop(
        0, heads * groups, one, jnp.zeros((2 * tokens, HD), jnp.float32), unroll=2
    )
    own_stat[...] = stat[:tokens]
    send_stat[...] = stat[tokens:]


def attend(chunk, live, own_q, other_q, new_kv, pieces):
    tokens = own_q.shape[0]
    groups = own_q.shape[1] // (KVH * HD)
    kw = HEADS_PER_CHUNK * HD
    qw = groups * kw
    nk = KVH // HEADS_PER_CHUNK
    keys = sum(p.shape[0] for p in pieces) + tokens
    f32, bf16 = jnp.float32, jnp.bfloat16
    shape = jax.ShapeDtypeStruct
    whole = lambda a: pl.BlockSpec(a.shape, lambda i: (0, 0))
    return pl.pallas_call(
        functools.partial(attend_kernel, groups),
        grid=(1,),
        out_shape=[
            shape((tokens, qw), f32),
            shape((tokens, HD), f32),
            shape((tokens, qw), bf16),
            shape((tokens, HD), f32),
        ],
        in_specs=[
            SMEM,
            pl.BlockSpec((tokens, qw), lambda i: (0, chunk)),
            pl.BlockSpec((tokens, qw), lambda i: (0, chunk)),
            pl.BlockSpec((tokens, kw), lambda i: (0, chunk)),
            pl.BlockSpec((tokens, kw), lambda i: (0, nk + chunk)),
        ]
        + [whole(p) for p in pieces],
        out_specs=[
            pl.BlockSpec((tokens, qw), lambda i: (0, 0)),
            pl.BlockSpec((tokens, HD), lambda i: (0, 0)),
            pl.BlockSpec((tokens, qw), lambda i: (0, 0)),
            pl.BlockSpec((tokens, HD), lambda i: (0, 0)),
        ],
        cost_estimate=pl.CostEstimate(
            flops=4 * 2 * tokens * keys * qw,
            bytes_accessed=2 * keys * 2 * kw + 12 * tokens * qw,
            transcendentals=2 * tokens * keys * qw // HD,
        ),
        name="attend",
    )(live, own_q, other_q, new_kv, new_kv, *pieces)


def merge_kernel(sum_a, stat_a, sum_b, stat_b, *rest):
    out = rest[-1]
    heads = out.shape[1] // HD
    factor = HD ** (-0.5) * math.log2(math.e)
    for head in range(heads):
        cols = slice(head * HD, (head + 1) * HD)
        high_a = stat_a[:, head : head + 1]
        high_b = stat_b[:, head : head + 1]
        total_a = stat_a[:, HD // 2 + head : HD // 2 + head + 1]
        total_b = stat_b[:, HD // 2 + head : HD // 2 + head + 1]
        largest = jnp.maximum(high_a, high_b)
        left = jnp.exp2((high_a - largest) * factor)
        right = jnp.exp2((high_b - largest) * factor)
        total = total_a * left + total_b * right
        top = sum_a[:, cols] * left + sum_b[:, cols].astype(jnp.float32) * right
        out[:, cols] = (top / total).astype(jnp.bfloat16)


def merge(chunk, mine, got, previous, columns):
    tokens, qw = mine[0].shape
    wide = pl.BlockSpec((tokens, qw), lambda i: (0, 0))
    thin = pl.BlockSpec((tokens, HD), lambda i: (0, 0))
    extra = [] if previous is None else [previous]
    return pl.pallas_call(
        merge_kernel,
        grid=(1,),
        out_shape=jax.ShapeDtypeStruct((tokens, columns), jnp.bfloat16),
        in_specs=[wide, thin, wide, thin] + [ANY] * len(extra),
        out_specs=pl.BlockSpec((tokens, qw), lambda i: (0, chunk)),
        input_output_aliases={4: 0} if extra else {},
        cost_estimate=pl.CostEstimate(
            flops=6 * tokens * qw, bytes_accessed=8 * tokens * qw, transcendentals=0
        ),
        name="merge",
    )(*mine, *got, *extra)


def on_device(old_cache, block_table, place_after, context_len, queries, new_kv):
    ninst = lax.axis_size("inst")
    ngroup = lax.axis_size("group")
    group_index = lax.axis_index("group")
    inst_index = lax.axis_index("inst")
    slots = old_cache.shape[1]
    blk = old_cache.shape[2]
    reqs = place_after.shape[0]
    nblk = block_table.shape[1]
    per_inst = nblk // ninst
    per_pair = slots // ngroup
    rgroup = ninst // 2
    cache = old_cache[0]

    other_q = lax.ppermute(queries, "inst", [(i, i ^ 1) for i in range(ninst)])

    columns = lax.dynamic_slice_in_dim(block_table, inst_index * per_inst, per_inst, 1)
    slot_ids = jnp.arange(reqs, dtype=jnp.int32)
    hit = place_after[None, :] == slot_ids[:, None]
    table = jnp.sum(jnp.where(hit[:, :, None], columns[None], 0), axis=1)
    table = table.reshape(ngroup, slots)
    owner = table // slots
    items = jnp.arange(slots, dtype=jnp.int32)
    before = items[:, None] < items[None, :]
    here = owner == group_index
    rank = jnp.sum(jnp.where(here[:, :, None] & before[None], 1, 0), axis=1)
    numbers = jnp.arange(per_pair, dtype=jnp.int32)
    chosen = here[:, None, :] & (rank[:, None, :] == numbers[None, :, None])
    send_slots = jnp.sum(jnp.where(chosen, (table % slots)[:, None, :], 0), axis=2)

    row = lax.dynamic_slice_in_dim(owner, group_index, 1, 0)[0]
    place = jnp.sum(jnp.where((row[:, None] == row[None, :]) & before, 1, 0), axis=0)
    order = ((row ^ group_index) * per_pair + place).reshape(rgroup, per_inst)

    even = inst_index % 2 == 0
    own = inst_index // 2
    which, sources, pairs = [own], [inst_index], []
    for d in range(1, ninst // 2):
        target = jnp.where((inst_index + d) % 2 == 0, inst_index + d, inst_index - d) % ninst
        which.append(target // 2)
        sources.append(jnp.where(even, inst_index - d, inst_index + d) % ninst)
        pairs.append(
            [((t - d) % ninst if t % 2 == 0 else (t + d) % ninst, t) for t in range(ninst)]
        )
    which = jnp.stack(which).astype(jnp.int32)
    own_slot = group_index * rgroup + own
    length = jnp.sum(jnp.where(place_after == own_slot, context_len, 0))
    span = per_inst * blk
    live = jnp.stack(
        [jnp.clip(length - s * span, 0, span) for s in sources] + [inst_index % 2]
    ).astype(jnp.int32)
    me = group_index.astype(jnp.int32).reshape(1)
    send_slots = send_slots.reshape(-1)

    chunks = KVH // HEADS_PER_CHUNK
    held = []
    for chunk in range(chunks):
        gate = held[chunk - 2][0] if chunk >= 2 else None
        outgoing = pack(chunk, send_slots, me, cache, ngroup, gate)
        arrived = [outgoing[0]] + [
            lax.ppermute(outgoing[step], "group", [(i, i ^ step) for i in range(ngroup)])
            for step in range(1, ngroup)
        ]
        pieces = unpack(order, which, arrived, blk, ninst // 2)
        held.append(
            [pieces[0]]
            + [lax.ppermute(p, "inst", pair) for p, pair in zip(pieces[1:], pairs)]
        )
    result = None
    for chunk in range(chunks):
        outs = attend(chunk, live, queries, other_q, new_kv, held[chunk])
        got = [lax.ppermute(o, "inst", [(i, i ^ 1) for i in range(ninst)]) for o in outs[2:]]
        result = merge(chunk, outs[:2], got, result, queries.shape[1])
    return result


def solution(mesh):
    return jax.shard_map(
        on_device,
        mesh=mesh,
        in_specs=(
            P("inst", "group", None, None),
            P(),
            P(),
            P(),
            P(("group", "inst"), None),
            P(("group", "inst"), None),
        ),
        out_specs=P(("group", "inst"), None),
        check_vma=False,
    )
```

```python
import functools
import math

import jax
import jax.numpy as jnp
from jax import lax
from jax.experimental import pallas as pl
from jax.experimental.pallas import tpu as pltpu
from jax.sharding import PartitionSpec as P


KVH = 8
HD = 128
NEG_FILL = -1e30
EARLY = 7
CHUNKS = (
    (0, 2, ((0, 2),), False),
    (2, 3, ((2, 2), (4, 1)), False),
    (5, 2, ((5, 1), (6, 1)), True),
)


SMEM = pl.BlockSpec(memory_space=pltpu.SMEM)
VMEM = pl.BlockSpec(memory_space=pltpu.VMEM)
ANY = pl.BlockSpec(memory_space=pl.ANY)
HBM = pl.BlockSpec(memory_space=pltpu.HBM)


def early_kernel(cache_ref, out, sems):
    for part in range(2):
        pltpu.make_async_copy(
            cache_ref.at[:, :, pl.ds((part * KVH + EARLY) * HD, HD)],
            out.at[:, :, pl.ds(part * HD, HD)],
            sems.at[part],
        ).start()
    for part in range(2):
        half = out.at[:, :, pl.ds(part * HD, HD)]
        pltpu.make_async_copy(half, half, sems.at[part]).wait()


def early(cache):
    slots, blk, _ = cache.shape
    return pl.pallas_call(
        early_kernel,
        out_shape=jax.ShapeDtypeStruct((slots, blk, 2 * HD), cache.dtype),
        in_specs=[HBM],
        out_specs=VMEM,
        scratch_shapes=[pltpu.SemaphoreType.DMA((2,))],
        cost_estimate=pl.CostEstimate(
            flops=0, bytes_accessed=8 * slots * blk * HD, transcendentals=0
        ),
        name="early",
        compiler_params=pltpu.CompilerParams(vmem_limit_bytes=62 << 20),
    )(cache)


def pack_kernel(first, heads, planes, steps, slots_ref, me_ref, *rest):
    sources, outs, sems = rest[: len(rest) - 1 - steps], rest[-1 - steps : -1], rest[-1]
    cache_ref = sources[0]
    blk = cache_ref.shape[1]
    per_pair = outs[0].shape[0] // blk
    slots = cache_ref.shape[0]
    me = me_ref[0]
    for step in range(steps):
        for item in range(per_pair):
            place = (me ^ step) * per_pair + item
            rows = pl.ds(item * blk, blk)
            slot = slots_ref[place]
            copies = [
                (cache_ref.at[slot, :, pl.ds((part * KVH + first) * HD, heads * HD)], part * heads, heads)
                for part in range(2)
            ]
            if planes:
                copies += [
                    (cache_ref.at[slot, :, pl.ds((part * KVH + EARLY) * HD, HD)], 2 * heads + part, 1)
                    for part in range(2)
                ]
            for plane in range(1, planes):
                moved = slots_ref[plane * slots + place]
                copies.append((sources[plane].at[moved], 2 * (heads + plane), 2))
            for source, at, wide in copies:
                pltpu.make_async_copy(
                    source, outs[step].at[rows, pl.ds(at * HD, wide * HD)], sems.at[step]
                ).start()
    for step in range(steps):
        pltpu.make_async_copy(outs[step], outs[step], sems.at[step]).wait()


def pack(first, heads, slots_table, me, cache, steps, moved):
    blk = cache.shape[1]
    per_pair = cache.shape[0] // steps
    planes = 1 + len(moved) if moved else 0
    piece = jax.ShapeDtypeStruct((per_pair * blk, 2 * (heads + planes) * HD), cache.dtype)
    return pl.pallas_call(
        functools.partial(pack_kernel, first, heads, planes, steps),
        out_shape=[piece] * steps,
        in_specs=[SMEM, SMEM, HBM] + [ANY] * len(moved),
        out_specs=[VMEM] * steps,
        scratch_shapes=[pltpu.SemaphoreType.DMA((steps,))],
        cost_estimate=pl.CostEstimate(
            flops=0, bytes_accessed=2 * steps * piece.size * 2, transcendentals=0
        ),
        name="pack",
        compiler_params=pltpu.CompilerParams(vmem_limit_bytes=62 << 20),
    )(slots_table, me, cache, *moved)


def unpack_kernel(steps, blk, ninst, plan, order_ref, me_ref, *rest):
    arrived = rest[:steps]
    outs = rest[steps:-2]
    held, sems = rest[-2:]
    rows = arrived[0].shape[0]
    slots = steps * rows // blk
    inst = me_ref[1]
    for step in range(steps):
        pltpu.make_async_copy(
            arrived[step], held.at[pl.ds(step * rows, rows)], sems.at[step]
        ).start()
    for step in range(steps):
        span = held.at[pl.ds(step * rows, rows)]
        pltpu.make_async_copy(span, span, sems.at[step]).wait()
    groups = {}
    for out, (plane, number, key, value, heads) in zip(outs, plan):
        groups.setdefault((plane, number), []).append((out, key, value, heads * HD))
    for (plane, number), members in groups.items():
        per_inst = members[0][0].shape[0] // blk
        target = inst + number
        if number:
            target = lax.rem(jnp.where(lax.rem(target, 2) == 0, target, inst - number + ninst), ninst)
        first = plane * slots + (target // 2) * per_inst
        for item in range(per_inst):
            source = pl.ds(pl.multiple_of(order_ref[first + item] * blk, blk), blk)
            here = slice(item * blk, (item + 1) * blk)
            for out, key, value, wide in members:
                out[here, :wide] = held[source, key * HD : key * HD + wide]
                out[here, wide:] = held[source, value * HD : value * HD + wide]


def unpack(order, me, arrived, blk, span, ninst, plan):
    steps = len(arrived)
    rows, width = arrived[0].shape
    return pl.pallas_call(
        functools.partial(unpack_kernel, steps, blk, ninst, plan),
        out_shape=[
            jax.ShapeDtypeStruct((span, 2 * entry[-1] * HD), arrived[0].dtype) for entry in plan
        ],
        in_specs=[SMEM, SMEM] + [ANY] * steps,
        out_specs=[VMEM] * len(plan),
        scratch_shapes=[
            pltpu.VMEM((steps * rows, width), arrived[0].dtype),
            pltpu.SemaphoreType.DMA((steps,)),
        ],
        cost_estimate=pl.CostEstimate(
            flops=0, bytes_accessed=4 * steps * rows * width, transcendentals=0
        ),
        name="unpack",
        compiler_params=pltpu.CompilerParams(vmem_limit_bytes=10 << 20),
    )(order, me, *arrived)


def attend_kernel(groups, ninst, local, remote, me_ref, place_ref, length_ref, *rest):
    rest = list(rest)
    own_q, other_q = rest[:2]
    new_k, new_v = rest[2:4] if local else (None, None)
    old_sum, old_stat = (None, None) if local else rest[2:4]
    numbers = list(range(0 if local else 1, ninst // 2 if remote else 1))
    pieces = rest[4 : 4 + len(numbers)]
    outs = rest[4 + len(numbers) :]
    tokens = own_q.shape[0]
    count = own_q.shape[1] // HD
    heads = count // groups
    factor = HD ** (-0.5) * math.log2(math.e)
    rows = pieces[0].shape[0]
    inst = me_ref[1]
    parity = lax.rem(inst, 2)
    slot = me_ref[0] * (ninst // 2) + inst // 2
    length = lax.fori_loop(
        0,
        place_ref.shape[0],
        lambda r, found: found + jnp.where(place_ref[r] == slot, length_ref[r], 0),
        0,
    )
    spots = lax.broadcasted_iota(jnp.int32, (1, rows), 1)
    fills = []
    for n in numbers:
        source = lax.rem(jnp.where(parity == 0, inst - n + ninst, inst + n), ninst)
        live = jnp.clip(length - source * rows, 0, rows)
        fills.append(jnp.where(spots < live, 0.0, NEG_FILL).astype(jnp.float32))
    if local:
        at_query = lax.broadcasted_iota(jnp.int32, (2 * tokens, tokens), 0)
        at_key = lax.broadcasted_iota(jnp.int32, (2 * tokens, tokens), 1)
        shift = jnp.where(parity == 0, 2 * tokens, -2 * tokens)
        reach = jnp.where(at_query < tokens, at_query, at_query + shift)
        fills.append(jnp.where(reach >= at_key, 0.0, NEG_FILL).astype(jnp.float32))
    lanes = lax.broadcasted_iota(jnp.int32, (2 * tokens, HD), 1)
    ones = jnp.ones((rows, HD), jnp.bfloat16)
    contract = (((1,), (1,)), ((), ()))

    def lane(number):
        return jnp.sum(jnp.where(lanes == number, old_stat[...], 0.0), axis=1, keepdims=True)

    def one(number, stat):
        head = number // groups
        qcol = pl.ds(pl.multiple_of(number * HD, HD), HD)
        kcol = pl.ds(pl.multiple_of(head * HD, HD), HD)
        vcol = pl.ds(pl.multiple_of((heads + head) * HD, HD), HD)
        query = jnp.concatenate([own_q[:, qcol], other_q[:, qcol]], axis=0)
        keys = [p[:, kcol] for p in pieces] + ([new_k[:, kcol]] if local else [])
        values = [p[:, vcol] for p in pieces] + ([new_v[:, kcol]] if local else [])
        scores = [
            lax.dot_general(query, k, contract, preferred_element_type=jnp.float32) + f
            for k, f in zip(keys, fills)
        ]
        peaks = [jnp.max(s, axis=1, keepdims=True) for s in scores]
        if not local:
            before = lane(number)
            peaks.append(before)
        largest = functools.reduce(jnp.maximum, peaks)
        total = None
        if not local:
            scale = jnp.exp2((before - largest) * factor)
            total = jnp.concatenate(
                [
                    old_sum[:, qcol] * scale,
                    jnp.broadcast_to(lane(count + number) * scale, (2 * tokens, HD)),
                ],
                axis=1,
            )
        for s, v in zip(scores, values):
            weight = jnp.exp2((s - largest) * factor).astype(jnp.bfloat16)
            wide = jnp.concatenate([v, ones[: v.shape[0]]], axis=1)
            part = jnp.dot(weight, wide, preferred_element_type=jnp.float32)
            total = part if total is None else total + part
        if remote:
            outs[0][:, qcol] = total[:tokens, :HD]
            outs[2][:, qcol] = total[tokens:, :HD].astype(jnp.bfloat16)
        else:
            outs[0][:, qcol] = total[:, :HD]
        stat = jnp.where(lanes == number, largest, stat)
        return jnp.where(lanes == count + number, total[:, HD:], stat)

    stat = lax.fori_loop(
        0, count, one, jnp.zeros((2 * tokens, HD), jnp.float32), unroll=groups
    )
    if not remote:
        outs[1][...] = stat
        return
    outs[1][...] = stat[:tokens]
    away = stat[tokens:]
    high = away.astype(jnp.bfloat16).astype(jnp.float32)
    middle = (away - high).astype(jnp.bfloat16).astype(jnp.float32)
    low = away - high - middle
    spread = high + pltpu.roll(middle, 2 * count, 1) + pltpu.roll(low, 4 * count, 1)
    outs[2][:, count * HD :] = spread.astype(jnp.bfloat16)


def attend(start, heads, scalars, own_q, other_q, new_kv, state, pieces, ninst, remote):
    local = state is None
    tokens = own_q.shape[0]
    groups = own_q.shape[1] // (KVH * HD)
    kw = heads * HD
    qw = groups * kw
    at = start // heads
    keys = sum(p.shape[0] for p in pieces) + tokens * local
    shape = jax.ShapeDtypeStruct
    whole = lambda r, c: pl.BlockSpec((r, c), lambda i: (0, 0))
    if remote:
        outs = [
            shape((tokens, qw), jnp.float32),
            shape((tokens, HD), jnp.float32),
            shape((tokens, qw + HD), jnp.bfloat16),
        ]
    else:
        outs = [shape((2 * tokens, qw), jnp.float32), shape((2 * tokens, HD), jnp.float32)]
    if local:
        extra = [new_kv, new_kv]
        specs = [
            pl.BlockSpec((tokens, kw), lambda i: (0, at)),
            pl.BlockSpec((tokens, kw), lambda i: (0, KVH // heads + at)),
        ]
    else:
        extra = list(state)
        specs = [whole(*a.shape) for a in extra]
    return pl.pallas_call(
        functools.partial(attend_kernel, groups, ninst, local, remote),
        grid=(1,),
        out_shape=outs,
        in_specs=[
            SMEM,
            SMEM,
            SMEM,
            pl.BlockSpec((tokens, qw), lambda i: (0, at)),
            pl.BlockSpec((tokens, qw), lambda i: (0, at)),
        ]
        + specs
        + [whole(*p.shape) for p in pieces],
        out_specs=[whole(*a.shape) for a in outs],
        cost_estimate=pl.CostEstimate(
            flops=4 * 2 * tokens * keys * qw,
            bytes_accessed=2 * keys * 2 * kw + 12 * tokens * qw,
            transcendentals=2 * tokens * keys * qw // HD,
        ),
        name="attend",
        compiler_params=pltpu.CompilerParams(vmem_limit_bytes=24 << 20),
    )(*scalars, own_q, other_q, *extra, *pieces)


def merge_kernel(own_sum, own_stat, got, *rest):
    out = rest[-1]
    count = out.shape[1] // HD
    factor = HD ** (-0.5) * math.log2(math.e)
    stat_a = own_stat[...]
    spread = got[:, count * HD :].astype(jnp.float32)
    stat_b = (
        spread
        + pltpu.roll(spread, HD - 2 * count, 1)
        + pltpu.roll(spread, HD - 4 * count, 1)
    )
    largest = jnp.maximum(stat_a, stat_b)
    left = jnp.exp2((stat_a - largest) * factor)
    right = jnp.exp2((stat_b - largest) * factor)
    total = (
        pltpu.roll(stat_a, HD - count, 1) * left + pltpu.roll(stat_b, HD - count, 1) * right
    )
    left, right = left / total, right / total
    for n in range(count):
        cols = slice(n * HD, (n + 1) * HD)
        top = own_sum[:, cols] * left[:, n : n + 1] + got[:, cols].astype(
            jnp.float32
        ) * right[:, n : n + 1]
        out[:, cols] = top.astype(jnp.bfloat16)


def merge(start, heads, mine, got, previous, columns):
    tokens, qw = mine[0].shape
    at = start // heads
    whole = lambda a: pl.BlockSpec(a.shape, lambda i: (0, 0))
    extra = [] if previous is None else [previous]
    return pl.pallas_call(
        merge_kernel,
        grid=(1,),
        out_shape=jax.ShapeDtypeStruct((tokens, columns), jnp.bfloat16),
        in_specs=[whole(a) for a in (*mine, got)] + [ANY] * len(extra),
        out_specs=pl.BlockSpec((tokens, qw), lambda i: (0, at)),
        input_output_aliases={3: 0} if extra else {},
        cost_estimate=pl.CostEstimate(
            flops=6 * tokens * qw, bytes_accessed=8 * tokens * qw, transcendentals=0
        ),
        name="merge",
        compiler_params=pltpu.CompilerParams(vmem_limit_bytes=6 << 20),
    )(*mine, got, *extra)


def on_device(old_cache, block_table, place_after, context_len, queries, new_kv):
    ninst = lax.axis_size("inst")
    ngroup = lax.axis_size("group")
    group_index = lax.axis_index("group")
    inst_index = lax.axis_index("inst")
    slots = old_cache.shape[1]
    blk = old_cache.shape[2]
    reqs = place_after.shape[0]
    nblk = block_table.shape[1]
    per_inst = nblk // ninst
    per_pair = slots // ngroup
    cache = old_cache[0]

    swap = [(i, i ^ 1) for i in range(ninst)]
    other_q = lax.ppermute(queries, "inst", swap)

    me = jnp.stack([group_index, inst_index]).astype(jnp.int32)
    even = inst_index % 2 == 0
    sources, pairs = [inst_index], []
    for d in range(1, ninst // 2):
        sources.append(jnp.where(even, inst_index - d, inst_index + d) % ninst)
        pairs.append(
            [((t - d) % ninst if t % 2 == 0 else (t + d) % ninst, t) for t in range(ninst)]
        )
    first_out = early(cache)
    slot_ids = jnp.arange(reqs, dtype=jnp.int32)
    hit = place_after[None, :] == slot_ids[:, None]
    items = jnp.arange(slots, dtype=jnp.int32)
    before = items[:, None] < items[None, :]
    numbers = jnp.arange(per_pair, dtype=jnp.int32)

    def lists(source):
        columns = lax.dynamic_slice_in_dim(block_table, source * per_inst, per_inst, 1)
        table = jnp.sum(jnp.where(hit[:, :, None], columns[None], 0), axis=1)
        table = table.reshape(ngroup, slots)
        owner = table // slots
        here = owner == group_index
        rank = jnp.sum(jnp.where(here[:, :, None] & before[None], 1, 0), axis=1)
        chosen = here[:, None, :] & (rank[:, None, :] == numbers[None, :, None])
        picked = jnp.sum(jnp.where(chosen, (table % slots)[:, None, :], 0), axis=2)
        row = lax.dynamic_slice_in_dim(owner, group_index, 1, 0)[0]
        place = jnp.sum(jnp.where((row[:, None] == row[None, :]) & before, 1, 0), axis=0)
        return picked.reshape(-1), (row ^ group_index) * per_pair + place

    own_lists = lists(inst_index)
    moved = [lax.ppermute(first_out, "inst", pair) for pair in pairs]
    more = [lists(source) for source in sources[1:]]
    every = [jnp.concatenate([own, *rest]) for own, *rest in zip(own_lists, *more)]

    held = []
    span = per_inst * blk
    for first, heads, runs, last in CHUNKS:
        picked, order = every if last else own_lists
        outgoing = pack(first, heads, picked, me, cache, ngroup, moved if last else [])
        arrived = [outgoing[0]] + [
            lax.ppermute(outgoing[step], "group", [(i, i ^ step) for i in range(ngroup)])
            for step in range(1, ngroup)
        ]
        plan = [
            (0, n, start - first, heads + start - first, count)
            for start, count in runs
            for n in range(ninst // 2)
        ]
        if last:
            plan += [
                (n, 0, 2 * (heads + n), 2 * (heads + n) + 1, 1) for n in range(ninst // 2)
            ]
        made = unpack(order, me, arrived, blk, span, ninst, tuple(plan))
        made = [made[at : at + ninst // 2] for at in range(0, len(made), ninst // 2)]
        if last:
            held.append((EARLY, 1, made.pop()))
        for (start, count), pieces in zip(runs, made):
            there = [lax.ppermute(p, "inst", pair) for p, pair in zip(pieces[1:], pairs)]
            held.append((start, count, [pieces[0]] + there))
    scalars = (me, place_after, context_len)
    result, waiting = None, []
    for number, (start, count, pieces) in enumerate(held):
        state, here = None, pieces
        if number not in TOGETHER:
            state = attend(
                start, count, scalars, queries, other_q, new_kv, None, pieces[:1], ninst, False
            )
            here = pieces[1:]
        outs = attend(
            start, count, scalars, queries, other_q, new_kv, state, here, ninst, True
        )
        got = lax.ppermute(outs[2], "inst", swap)
        waiting.append((start, count, outs[:2], got))
    for number in MERGES:
        start, count, mine, got = waiting[number]
        result = merge(start, count, mine, got, result, queries.shape[1])
    return result


TOGETHER = (3,)
MERGES = (3, 0, 1, 2, 4, 5)


def solution(mesh):
    return jax.shard_map(
        on_device,
        mesh=mesh,
        in_specs=(
            P("inst", "group", None, None),
            P(),
            P(),
            P(),
            P(("group", "inst"), None),
            P(("group", "inst"), None),
        ),
        out_specs=P(("group", "inst"), None),
        check_vma=False,
    )
```

```python
import functools
import math

import jax
import jax.numpy as jnp
from jax import lax
from jax.experimental import pallas as pl
from jax.experimental.pallas import tpu as pltpu
from jax.sharding import PartitionSpec as P


KVH = 8
HD = 128
NEG_FILL = -1e30
EARLY = 7
CHUNKS = (
    (0, 2, ((0, 2),), False),
    (2, 3, ((2, 2), (4, 1)), False),
    (5, 2, ((5, 1), (6, 1)), True),
)


SMEM = pl.BlockSpec(memory_space=pltpu.SMEM)
VMEM = pl.BlockSpec(memory_space=pltpu.VMEM)
ANY = pl.BlockSpec(memory_space=pl.ANY)
HBM = pl.BlockSpec(memory_space=pltpu.HBM)


def early_kernel(cache_ref, out, sems):
    for part in range(2):
        pltpu.make_async_copy(
            cache_ref.at[:, :, pl.ds((part * KVH + EARLY) * HD, HD)],
            out.at[:, :, pl.ds(part * HD, HD)],
            sems.at[part],
        ).start()
    for part in range(2):
        half = out.at[:, :, pl.ds(part * HD, HD)]
        pltpu.make_async_copy(half, half, sems.at[part]).wait()


def early(cache):
    slots, blk, _ = cache.shape
    return pl.pallas_call(
        early_kernel,
        out_shape=jax.ShapeDtypeStruct((slots, blk, 2 * HD), cache.dtype),
        in_specs=[HBM],
        out_specs=VMEM,
        scratch_shapes=[pltpu.SemaphoreType.DMA((2,))],
        cost_estimate=pl.CostEstimate(
            flops=0, bytes_accessed=8 * slots * blk * HD, transcendentals=0
        ),
        name="early",
        compiler_params=pltpu.CompilerParams(vmem_limit_bytes=62 << 20),
    )(cache)


def pack_kernel(first, heads, planes, steps, slots_ref, me_ref, *rest):
    sources, outs, sems = rest[: len(rest) - 1 - steps], rest[-1 - steps : -1], rest[-1]
    cache_ref = sources[0]
    blk = cache_ref.shape[1]
    per_pair = outs[0].shape[0] // blk
    slots = cache_ref.shape[0]
    me = me_ref[0]
    for step in range(steps):
        for item in range(per_pair):
            place = (me ^ step) * per_pair + item
            rows = pl.ds(item * blk, blk)
            slot = slots_ref[place]
            copies = [
                (cache_ref.at[slot, :, pl.ds((part * KVH + first) * HD, heads * HD)], part * heads, heads)
                for part in range(2)
            ]
            if planes:
                copies += [
                    (cache_ref.at[slot, :, pl.ds((part * KVH + EARLY) * HD, HD)], 2 * heads + part, 1)
                    for part in range(2)
                ]
            for plane in range(1, planes):
                moved = slots_ref[plane * slots + place]
                copies.append((sources[plane].at[moved], 2 * (heads + plane), 2))
            for source, at, wide in copies:
                pltpu.make_async_copy(
                    source, outs[step].at[rows, pl.ds(at * HD, wide * HD)], sems.at[step]
                ).start()
    for step in range(steps):
        pltpu.make_async_copy(outs[step], outs[step], sems.at[step]).wait()


def pack(first, heads, slots_table, me, cache, steps, moved):
    blk = cache.shape[1]
    per_pair = cache.shape[0] // steps
    planes = 1 + len(moved) if moved else 0
    piece = jax.ShapeDtypeStruct((per_pair * blk, 2 * (heads + planes) * HD), cache.dtype)
    return pl.pallas_call(
        functools.partial(pack_kernel, first, heads, planes, steps),
        out_shape=[piece] * steps,
        in_specs=[SMEM, SMEM, HBM] + [ANY] * len(moved),
        out_specs=[VMEM] * steps,
        scratch_shapes=[pltpu.SemaphoreType.DMA((steps,))],
        cost_estimate=pl.CostEstimate(
            flops=0, bytes_accessed=2 * steps * piece.size * 2, transcendentals=0
        ),
        name="pack",
        compiler_params=pltpu.CompilerParams(vmem_limit_bytes=62 << 20),
    )(slots_table, me, cache, *moved)


def unpack_kernel(steps, blk, ninst, plan, order_ref, me_ref, *rest):
    arrived = rest[:steps]
    outs = rest[steps:-2]
    held, sems = rest[-2:]
    rows = arrived[0].shape[0]
    slots = steps * rows // blk
    inst = me_ref[1]
    for step in range(steps):
        pltpu.make_async_copy(
            arrived[step], held.at[pl.ds(step * rows, rows)], sems.at[step]
        ).start()
    for step in range(steps):
        span = held.at[pl.ds(step * rows, rows)]
        pltpu.make_async_copy(span, span, sems.at[step]).wait()
    groups = {}
    for out, (plane, number, key, value, heads) in zip(outs, plan):
        groups.setdefault((plane, number), []).append((out, key, value, heads * HD))
    for (plane, number), members in groups.items():
        per_inst = members[0][0].shape[0] // blk
        target = inst + number
        if number:
            target = lax.rem(jnp.where(lax.rem(target, 2) == 0, target, inst - number + ninst), ninst)
        first = plane * slots + (target // 2) * per_inst
        for item in range(per_inst):
            source = pl.ds(pl.multiple_of(order_ref[first + item] * blk, blk), blk)
            here = slice(item * blk, (item + 1) * blk)
            for out, key, value, wide in members:
                out[here, :wide] = held[source, key * HD : key * HD + wide]
                out[here, wide:] = held[source, value * HD : value * HD + wide]


def unpack(order, me, arrived, blk, span, ninst, room, plan):
    steps = len(arrived)
    rows, width = arrived[0].shape
    return pl.pallas_call(
        functools.partial(unpack_kernel, steps, blk, ninst, plan),
        out_shape=[
            jax.ShapeDtypeStruct((span, 2 * entry[-1] * HD), arrived[0].dtype) for entry in plan
        ],
        in_specs=[SMEM, SMEM] + [ANY] * steps,
        out_specs=[VMEM] * len(plan),
        scratch_shapes=[
            pltpu.VMEM((steps * rows, width), arrived[0].dtype),
            pltpu.SemaphoreType.DMA((steps,)),
        ],
        cost_estimate=pl.CostEstimate(
            flops=0, bytes_accessed=4 * steps * rows * width, transcendentals=0
        ),
        name="unpack",
        compiler_params=pltpu.CompilerParams(vmem_limit_bytes=room << 20),
    )(order, me, *arrived)


def attend_kernel(groups, ninst, local, remote, me_ref, place_ref, length_ref, *rest):
    rest = list(rest)
    own_q, other_q = rest[:2]
    new_k, new_v = rest[2:4] if local else (None, None)
    old_sum, old_stat = (None, None) if local else rest[2:4]
    numbers = list(range(0 if local else 1, ninst // 2 if remote else 1))
    pieces = rest[4 : 4 + len(numbers)]
    outs = rest[4 + len(numbers) :]
    tokens = own_q.shape[0]
    count = own_q.shape[1] // HD
    heads = count // groups
    factor = HD ** (-0.5) * math.log2(math.e)
    rows = pieces[0].shape[0]
    inst = me_ref[1]
    parity = lax.rem(inst, 2)
    slot = me_ref[0] * (ninst // 2) + inst // 2
    length = lax.fori_loop(
        0,
        place_ref.shape[0],
        lambda r, found: found + jnp.where(place_ref[r] == slot, length_ref[r], 0),
        0,
    )
    spots = lax.broadcasted_iota(jnp.int32, (1, rows), 1)
    fills = []
    for n in numbers:
        source = lax.rem(jnp.where(parity == 0, inst - n + ninst, inst + n), ninst)
        live = jnp.clip(length - source * rows, 0, rows)
        fills.append(jnp.where(spots < live, 0.0, NEG_FILL).astype(jnp.float32))
    if local:
        at_query = lax.broadcasted_iota(jnp.int32, (2 * tokens, tokens), 0)
        at_key = lax.broadcasted_iota(jnp.int32, (2 * tokens, tokens), 1)
        shift = jnp.where(parity == 0, 2 * tokens, -2 * tokens)
        reach = jnp.where(at_query < tokens, at_query, at_query + shift)
        fills.append(jnp.where(reach >= at_key, 0.0, NEG_FILL).astype(jnp.float32))
    lanes = lax.broadcasted_iota(jnp.int32, (2 * tokens, HD), 1)
    ones = jnp.ones((rows, HD), jnp.bfloat16)
    contract = (((1,), (1,)), ((), ()))

    def lane(number):
        return jnp.sum(jnp.where(lanes == number, old_stat[...], 0.0), axis=1, keepdims=True)

    def one(number, stat):
        head = number // groups
        qcol = pl.ds(pl.multiple_of(number * HD, HD), HD)
        kcol = pl.ds(pl.multiple_of(head * HD, HD), HD)
        vcol = pl.ds(pl.multiple_of((heads + head) * HD, HD), HD)
        query = jnp.concatenate([own_q[:, qcol], other_q[:, qcol]], axis=0)
        keys = [p[:, kcol] for p in pieces] + ([new_k[:, kcol]] if local else [])
        values = [p[:, vcol] for p in pieces] + ([new_v[:, kcol]] if local else [])
        scores = [
            lax.dot_general(query, k, contract, preferred_element_type=jnp.float32) + f
            for k, f in zip(keys, fills)
        ]
        peaks = [jnp.max(s, axis=1, keepdims=True) for s in scores]
        if not local:
            before = lane(number)
            peaks.append(before)
        largest = functools.reduce(jnp.maximum, peaks)
        total = None
        if not local:
            scale = jnp.exp2((before - largest) * factor)
            total = jnp.concatenate(
                [
                    old_sum[:, qcol] * scale,
                    jnp.broadcast_to(lane(count + number) * scale, (2 * tokens, HD)),
                ],
                axis=1,
            )
        for s, v in zip(scores, values):
            weight = jnp.exp2((s - largest) * factor).astype(jnp.bfloat16)
            wide = jnp.concatenate([v, ones[: v.shape[0]]], axis=1)
            part = jnp.dot(weight, wide, preferred_element_type=jnp.float32)
            total = part if total is None else total + part
        if remote:
            outs[0][:, qcol] = total[:tokens, :HD]
            outs[2][:, qcol] = total[tokens:, :HD].astype(jnp.bfloat16)
        else:
            outs[0][:, qcol] = total[:, :HD]
        stat = jnp.where(lanes == number, largest, stat)
        return jnp.where(lanes == count + number, total[:, HD:], stat)

    stat = lax.fori_loop(
        0, count, one, jnp.zeros((2 * tokens, HD), jnp.float32), unroll=groups
    )
    if not remote:
        outs[1][...] = stat
        return
    outs[1][...] = stat[:tokens]
    away = stat[tokens:]
    high = away.astype(jnp.bfloat16).astype(jnp.float32)
    middle = (away - high).astype(jnp.bfloat16).astype(jnp.float32)
    low = away - high - middle
    spread = high + pltpu.roll(middle, 2 * count, 1) + pltpu.roll(low, 4 * count, 1)
    outs[2][:, count * HD :] = spread.astype(jnp.bfloat16)


def attend(start, heads, scalars, own_q, other_q, new_kv, state, pieces, ninst, remote):
    local = state is None
    tokens = own_q.shape[0]
    groups = own_q.shape[1] // (KVH * HD)
    kw = heads * HD
    qw = groups * kw
    at = start // heads
    keys = sum(p.shape[0] for p in pieces) + tokens * local
    shape = jax.ShapeDtypeStruct
    whole = lambda r, c: pl.BlockSpec((r, c), lambda i: (0, 0))
    if remote:
        outs = [
            shape((tokens, qw), jnp.float32),
            shape((tokens, HD), jnp.float32),
            shape((tokens, qw + HD), jnp.bfloat16),
        ]
    else:
        outs = [shape((2 * tokens, qw), jnp.float32), shape((2 * tokens, HD), jnp.float32)]
    if local:
        extra = [new_kv, new_kv]
        specs = [
            pl.BlockSpec((tokens, kw), lambda i: (0, at)),
            pl.BlockSpec((tokens, kw), lambda i: (0, KVH // heads + at)),
        ]
    else:
        extra = list(state)
        specs = [whole(*a.shape) for a in extra]
    return pl.pallas_call(
        functools.partial(attend_kernel, groups, ninst, local, remote),
        grid=(1,),
        out_shape=outs,
        in_specs=[
            SMEM,
            SMEM,
            SMEM,
            pl.BlockSpec((tokens, qw), lambda i: (0, at)),
            pl.BlockSpec((tokens, qw), lambda i: (0, at)),
        ]
        + specs
        + [whole(*p.shape) for p in pieces],
        out_specs=[whole(*a.shape) for a in outs],
        cost_estimate=pl.CostEstimate(
            flops=4 * 2 * tokens * keys * qw,
            bytes_accessed=2 * keys * 2 * kw + 12 * tokens * qw,
            transcendentals=2 * tokens * keys * qw // HD,
        ),
        name="attend",
        compiler_params=pltpu.CompilerParams(vmem_limit_bytes=24 << 20),
    )(*scalars, own_q, other_q, *extra, *pieces)


def merge_kernel(own_sum, own_stat, got, *rest):
    out = rest[-1]
    count = out.shape[1] // HD
    factor = HD ** (-0.5) * math.log2(math.e)
    stat_a = own_stat[...]
    spread = got[:, count * HD :].astype(jnp.float32)
    stat_b = (
        spread
        + pltpu.roll(spread, HD - 2 * count, 1)
        + pltpu.roll(spread, HD - 4 * count, 1)
    )
    largest = jnp.maximum(stat_a, stat_b)
    left = jnp.exp2((stat_a - largest) * factor)
    right = jnp.exp2((stat_b - largest) * factor)
    total = (
        pltpu.roll(stat_a, HD - count, 1) * left + pltpu.roll(stat_b, HD - count, 1) * right
    )
    left, right = left / total, right / total
    for n in range(count):
        cols = slice(n * HD, (n + 1) * HD)
        top = own_sum[:, cols] * left[:, n : n + 1] + got[:, cols].astype(
            jnp.float32
        ) * right[:, n : n + 1]
        out[:, cols] = top.astype(jnp.bfloat16)


def merge(start, heads, mine, got, previous, columns):
    tokens, qw = mine[0].shape
    at = start // heads
    whole = lambda a: pl.BlockSpec(a.shape, lambda i: (0, 0))
    extra = [] if previous is None else [previous]
    return pl.pallas_call(
        merge_kernel,
        grid=(1,),
        out_shape=jax.ShapeDtypeStruct((tokens, columns), jnp.bfloat16),
        in_specs=[whole(a) for a in (*mine, got)] + [ANY] * len(extra),
        out_specs=pl.BlockSpec((tokens, qw), lambda i: (0, at)),
        input_output_aliases={3: 0} if extra else {},
        cost_estimate=pl.CostEstimate(
            flops=6 * tokens * qw, bytes_accessed=8 * tokens * qw, transcendentals=0
        ),
        name="merge",
        compiler_params=pltpu.CompilerParams(vmem_limit_bytes=6 << 20),
    )(*mine, got, *extra)


def on_device(old_cache, block_table, place_after, context_len, queries, new_kv):
    ninst = lax.axis_size("inst")
    ngroup = lax.axis_size("group")
    group_index = lax.axis_index("group")
    inst_index = lax.axis_index("inst")
    slots = old_cache.shape[1]
    blk = old_cache.shape[2]
    reqs = place_after.shape[0]
    nblk = block_table.shape[1]
    per_inst = nblk // ninst
    per_pair = slots // ngroup
    cache = old_cache[0]

    swap = [(i, i ^ 1) for i in range(ninst)]
    other_q = lax.ppermute(queries, "inst", swap)

    me = jnp.stack([group_index, inst_index]).astype(jnp.int32)
    even = inst_index % 2 == 0
    sources, pairs = [inst_index], []
    for d in range(1, ninst // 2):
        sources.append(jnp.where(even, inst_index - d, inst_index + d) % ninst)
        pairs.append(
            [((t - d) % ninst if t % 2 == 0 else (t + d) % ninst, t) for t in range(ninst)]
        )
    first_out = early(cache)
    slot_ids = jnp.arange(reqs, dtype=jnp.int32)
    hit = place_after[None, :] == slot_ids[:, None]
    items = jnp.arange(slots, dtype=jnp.int32)
    before = items[:, None] < items[None, :]
    numbers = jnp.arange(per_pair, dtype=jnp.int32)

    def lists(source):
        columns = lax.dynamic_slice_in_dim(block_table, source * per_inst, per_inst, 1)
        table = jnp.sum(jnp.where(hit[:, :, None], columns[None], 0), axis=1)
        table = table.reshape(ngroup, slots)
        owner = table // slots
        here = owner == group_index
        rank = jnp.sum(jnp.where(here[:, :, None] & before[None], 1, 0), axis=1)
        chosen = here[:, None, :] & (rank[:, None, :] == numbers[None, :, None])
        picked = jnp.sum(jnp.where(chosen, (table % slots)[:, None, :], 0), axis=2)
        row = lax.dynamic_slice_in_dim(owner, group_index, 1, 0)[0]
        place = jnp.sum(jnp.where((row[:, None] == row[None, :]) & before, 1, 0), axis=0)
        return picked.reshape(-1), (row ^ group_index) * per_pair + place

    own_lists = lists(inst_index)
    moved = [lax.ppermute(first_out, "inst", pair) for pair in pairs]
    held = []
    span = per_inst * blk
    for number, (first, heads, runs, last) in enumerate(CHUNKS):
        picked, order = own_lists
        if last:
            more = [lists(source) for source in sources]
            picked, order = [jnp.concatenate([own, *rest]) for own, *rest in zip(own_lists, *more)]
        outgoing = pack(first, heads, picked, me, cache, ngroup, moved if last else [])
        arrived = [outgoing[0]] + [
            lax.ppermute(outgoing[step], "group", [(i, i ^ step) for i in range(ngroup)])
            for step in range(1, ngroup)
        ]
        plan = [
            (0, n, start - first, heads + start - first, count)
            for start, count in runs
            for n in range(ninst // 2)
        ]
        if last:
            plan += [
                (n, 0, 2 * (heads + n), 2 * (heads + n) + 1, 1) for n in range(ninst // 2)
            ]
        room = 62 if number == 0 else 10
        sort = functools.partial(unpack, order, me, arrived, blk, span, ninst, room)
        if number == 0:
            going = tuple(entry for entry in plan if entry[1])
            sent = iter(sort(going))
            stay = iter(sort(tuple(entry for entry in plan if not entry[1])))
            made = [next(sent) if entry[1] else next(stay) for entry in plan]
            sources, _ = lax.optimization_barrier((sources[1:], made[1]))
        else:
            made = sort(tuple(plan))
        made = [made[at : at + ninst // 2] for at in range(0, len(made), ninst // 2)]
        if last:
            held.append((EARLY, 1, made.pop()))
        for (start, count), pieces in zip(runs, made):
            there = [lax.ppermute(p, "inst", pair) for p, pair in zip(pieces[1:], pairs)]
            held.append((start, count, [pieces[0]] + there))
    scalars = (me, place_after, context_len)
    result, waiting = None, []
    for number, (start, count, pieces) in enumerate(held):
        state, here = None, pieces
        if number not in TOGETHER:
            state = attend(
                start, count, scalars, queries, other_q, new_kv, None, pieces[:1], ninst, False
            )
            here = pieces[1:]
        outs = attend(
            start, count, scalars, queries, other_q, new_kv, state, here, ninst, True
        )
        got = lax.ppermute(outs[2], "inst", swap)
        waiting.append((start, count, outs[:2], got))
    for number in MERGES:
        start, count, mine, got = waiting[number]
        result = merge(start, count, mine, got, result, queries.shape[1])
    return result


TOGETHER = (3,)
MERGES = (3, 0, 1, 2, 4, 5)


def solution(mesh):
    return jax.shard_map(
        on_device,
        mesh=mesh,
        in_specs=(
            P("inst", "group", None, None),
            P(),
            P(),
            P(),
            P(("group", "inst"), None),
            P(("group", "inst"), None),
        ),
        out_specs=P(("group", "inst"), None),
        check_vma=False,
    )
```
